32 devices in a mesh: dp: 16 (over z, x, core), shard: 2 (over y).
Axes of the slice: x: 2, y: 2, z: 4, core: 2. Of those that a mesh axis runs over, the one named last changes fastest.
Arguments:
- hidden_in: bfloat16 [4096, 1024], P(('dp', 'shard')), may hold values from -8 to 8
- segments: int32 [16, 256], P('dp', 'shard'), may hold values from 0 to 2, never falling along the last dimension, each value on 1 to 128 neighbouring positions
- routes: int32 [4096, 8], P(('dp', 'shard')), may hold values from 0 to 15, all different within a row; in each aligned block of 128 rows (0 to 127, 128 to 255, ...) at most 68 rows name the same one
- cotangent: bfloat16 [4096, 1024], P(('dp', 'shard')), may hold values from -6 to 6
- norm_gains: float32 [2, 1024], P(None, 'dp'), may hold values from 0.5 to 1.5
- gains_moment: float32 [2, 1024], P(None, 'dp'), may hold values from -192 to 192
- gains_square: float32 [2, 1024], P(None, 'dp'), may hold values from 800 to 4000
- w_qkv: float32 [1024, 2048], P('dp'), may hold values from -1 to 1
- qkv_moment: float32 [1024, 2048], P('dp'), may hold values from -128 to 128
- qkv_square: float32 [1024, 2048], P('dp'), may hold values from 340 to 1700
- w_out: float32 [1024, 1024], P('dp'), may hold values from -1.5 to 1.5
- out_moment: float32 [1024, 1024], P('dp'), may hold values from -32 to 32
- out_square: float32 [1024, 1024], P('dp'), may hold values from 26 to 130
- w_router: float32 [1024, 16], P('dp'), may hold values from -3 to 3
- router_moment: float32 [1024, 16], P('dp'), may hold values from -896 to 896
- router_square: float32 [1024, 16], P('dp'), may hold values from 20000 to 100000
- w_gate_up: float32 [16, 1024, 1024], P('dp', 'shard'), may hold values from -0.1875 to 0.1875
- gate_up_moment: float32 [16, 1024, 1024], P('dp', 'shard'), may hold values from -40 to 40
- gate_up_square: float32 [16, 1024, 1024], P('dp', 'shard'), may hold values from 40 to 200
- w_down: float32 [16, 512, 1024], P('dp', 'shard'), may hold values from -1 to 1
- down_moment: float32 [16, 512, 1024], P('dp', 'shard'), may hold values from -6 to 6
- down_square: float32 [16, 512, 1024], P('dp', 'shard'), may hold values from 1 to 5
Outputs:
- block_out: bfloat16 [4096, 1024], P(('dp', 'shard'))
- input_grad: float32 [4096, 1024], P(('dp', 'shard'))
- gains_grad: float32 [2, 1024], P(None, 'dp')
- qkv_grad: float32 [1024, 2048], P('dp')
- out_grad: float32 [1024, 1024], P('dp')
- router_grad: float32 [1024, 16], P('dp')
- gate_up_grad: float32 [16, 1024, 1024], P('dp', 'shard')
- down_grad: float32 [16, 512, 1024], P('dp', 'shard')
- new_gains: float32 [2, 1024], P(None, 'dp')
- new_gains_moment: float32 [2, 1024], P(None, 'dp')
- new_gains_square: float32 [2, 1024], P(None, 'dp')
- new_qkv: float32 [1024, 2048], P('dp')
- new_qkv_moment: float32 [1024, 2048], P('dp')
- new_qkv_square: float32 [1024, 2048], P('dp')
- new_out: float32 [1024, 1024], P('dp')
- new_out_moment: float32 [1024, 1024], P('dp')
- new_out_square: float32 [1024, 1024], P('dp')
- new_router: float32 [1024, 16], P('dp')
- new_router_moment: float32 [1024, 16], P('dp')
- new_router_square: float32 [1024, 16], P('dp')
- new_gate_up: float32 [16, 1024, 1024], P('dp', 'shard')
- new_gate_up_moment: float32 [16, 1024, 1024], P('dp', 'shard')
- new_gate_up_square: float32 [16, 1024, 1024], P('dp', 'shard')
- new_down: float32 [16, 512, 1024], P('dp', 'shard')
- new_down_moment: float32 [16, 512, 1024], P('dp', 'shard')
- new_down_square: float32 [16, 512, 1024], P('dp', 'shard')
The draws below stay inside these ranges and needn't reach their ends.
Inputs may be any that keep to these rules, and one draw needn't show every extreme that they name: `segments`: document numbers never fall along a sequence; each document holds 1 to 128 positions and one holds exactly 128. `routes`: each row names 8 different experts. Within the 128 rows of one device no expert is named by more than 68 rows, a bound that some block reaches; every expert is named somewhere.
All inputs are finite; a program needn't handle non-finite values.
Results may differ from the reference program's by a relative error of at most 0.035.
The reference program's roundings to bfloat16 on the way count: a program that leaves them out, or rounds other values in their place, can miss the bound.
Values may be sent and summed in bfloat16 or wider, within the bound.
No kernel may reach another device: no remote copies, remote signals or barrier semaphores. Data moves between devices by JAX's collectives and lax.ppermute only.
A program may use at most 128 MiB of HBM per device.

```python
import math
import jax
import jax.numpy as jnp
import numpy as np
from jax import lax

D = 1024
HQ = 16
HK = 8
HD = 64
FF = 512
TOP = 8
TOK_DEV = 128
SEGS = 3
STEP = 3
EXPERTS = 16
LENGTH = 256
SEQS = 16
TOKENS = 4096
CAP = 68
SEG_MOST = 128
QKV = 2048


def draw_hidden_in(key, part):
    values = jax.random.normal(jax.random.fold_in(key, 15), (TOKENS, D), jnp.float32)
    return jnp.clip(values, -8.0, 8.0).astype(jnp.bfloat16)


def draw_w_qkv(key, part):
    columns = (HQ + 2 * HK) * HD
    base_weight = jnp.clip(jax.random.normal(jax.random.fold_in(key, 21), (D, columns), jnp.float32), -4.0, 4.0) * D ** (-0.5)
    return base_weight


def draw_w_router(key, part):
    base_weight = jnp.clip(jax.random.normal(jax.random.fold_in(key, 31), (D, EXPERTS), jnp.float32), -4.0, 4.0) * D ** (-0.5)
    return base_weight


def level_of(stream_key, shape, shards, smallest, top_value):
    loudness, own = 1.0, jax.random.fold_in(stream_key, 6)
    for position, parts in shards:
        draws = jnp.exp(jax.random.uniform(jax.random.fold_in(own, position), (parts,), jnp.float32, smallest / len(shards), top_value / len(shards)))
        loudness = loudness * jnp.repeat(draws, shape[position] // parts).reshape([-1 if axis == position else 1 for axis in range(len(shape))])
    return loudness


def split_up(count, total, bound, lean):
    loads = [(1 << 20) // math.isqrt(standing ** lean) + 1 for standing in range(2, count + 1)]
    surplus, counts = total - bound - (count - 1), [1] * (count - 1)
    while surplus > 0:
        movable = [i for i in range(count - 1) if counts[i] < bound]
        mass, remaining = sum([loads[i] for i in movable]), surplus
        for i in movable:
            more = min(bound - counts[i], max(1, remaining * loads[i] // mass), surplus)
            counts[i] = counts[i] + more
            surplus = surplus - more
    return np.array([bound] + counts)


def ragged(own_key, number_of, total, most, lean):
    if number_of == 2:
        one = jax.random.randint(own_key, (), max(1, total - most), min(most, total - 1) + 1)
        return jnp.stack([one, total - one])
    tallies = jnp.asarray(split_up(number_of, total, most, lean), jnp.int32)
    pairs = (number_of - 1) // 2
    donor, taker = tallies[1:1 + 2 * pairs:2], tallies[2:2 + 2 * pairs:2]
    slack = jnp.minimum(donor - 1, most - taker)
    moved = jax.random.randint(jax.random.fold_in(own_key, 1), (pairs,), 0, 1 << 20) % (slack + 1)
    tallies = tallies.at[1:1 + 2 * pairs:2].set(donor - moved).at[2:2 + 2 * pairs:2].set(taker + moved)
    return tallies[jax.random.permutation(jax.random.fold_in(own_key, 2), number_of)]


def shared_out(stream_key, own, number, rows, amount, top, reach, skew):
    sequence = jax.random.permutation(stream_key, amount)
    crowded, ordinary = load_shares(amount, rows * top, reach, skew, True), load_shares(amount, rows * top, reach, skew, False)
    places = jnp.arange(amount)

    def named(lengths, rotation):
        used = int((lengths > 0).sum())
        fixed = max(1, used // 4)
        shifted = fixed + (places - fixed + rotation * (used - fixed)) % max(1, amount - fixed)
        return jnp.zeros((amount,), jnp.int32).at[sequence[jnp.where(places < fixed, places, shifted)]].set(jnp.asarray(lengths, jnp.int32))

    lengths = jnp.where(number % 4 == 0, named(crowded, number // 4), named(ordinary, number - number // 4 - 1))
    mixed = jax.random.permutation(jax.random.fold_in(own, 3), amount)
    source_of, receiver = mixed[0:amount // 2 * 2:2], mixed[1:amount // 2 * 2:2]
    slack = jnp.minimum(lengths[source_of] - 1, reach - lengths[receiver]) // 2
    slack = jnp.where((source_of == sequence[0]) | (receiver == sequence[0]) | (lengths[receiver] == 0), 0, jnp.maximum(slack, 0))
    shifted = jax.random.randint(jax.random.fold_in(own, 4), (amount // 2,), 0, 1 << 20) % (slack + 1)
    lengths = lengths.at[source_of].add(-shifted).at[receiver].add(shifted)
    labels = jnp.searchsorted(jnp.cumsum(lengths), jnp.arange(rows * top), side="right").astype(jnp.int32)
    listing = labels.reshape(top, rows).T
    listing = listing[jax.random.permutation(jax.random.fold_in(own, 1), rows)]
    rotation = jax.random.randint(jax.random.fold_in(own, 2), (rows, 1), 0, top)
    return jnp.take_along_axis(listing, (jnp.arange(top)[None, :] + rotation) % top, axis=1)


def load_shares(count, total, most, slope, full):
    portions = [(1 << 20) // math.isqrt(rank ** slope) + 1 for rank in range(1, count + 1)]
    largest = most if full else min(most, max(-(-total // count), total * portions[0] // sum(portions)))
    least = 1 if total - largest >= count - 1 else 0
    given, surplus = [largest] + [least] * (count - 1), total - largest - least * (count - 1)
    while surplus > 0:
        movable = [i for i in range(1, count) if given[i] < largest] or [i for i in range(1, count) if given[i] < most]
        mass, remaining = sum([portions[i] for i in movable]), surplus
        for i in movable:
            extra = min(most - given[i], max(1, remaining * portions[i] // mass), surplus)
            given[i] = given[i] + extra
            surplus = surplus - extra
    return np.array(given)


def bell_draw(key, shape, width, limit, cuts=(), kind=jnp.bfloat16):
    array = width * jax.random.normal(key, shape, jnp.float32)
    if cuts:
        array = array * level_of(key, shape, cuts, -0.22, 0.18)
    return jnp.clip(array, -limit, limit).astype(kind)


def setup_inputs(seed: int = 0) -> dict:
    splits = jax.random.split(jax.random.key(seed), 23)
    hidden_in = draw_hidden_in(jax.random.fold_in(splits[22], 71), 0)
    segments = jax.vmap(lambda own: jnp.searchsorted(jnp.cumsum(ragged(own, SEGS, LENGTH, SEG_MOST, 1)), jnp.arange(LENGTH), side="right"))(jax.random.split(splits[1], SEQS)).reshape((SEQS, LENGTH)).astype(jnp.int32)
    routes_keys = jax.random.split(jax.random.fold_in(splits[2], 1), TOKENS // TOK_DEV)
    routes_turns = jax.random.permutation(jax.random.fold_in(splits[2], 3), TOKENS // TOK_DEV)
    routes = jax.vmap(lambda own, number: shared_out(jax.random.fold_in(splits[2], 2), own, number, TOK_DEV, EXPERTS, TOP, CAP, 1))(routes_keys, routes_turns).reshape((TOKENS, TOP))
    cotangent = bell_draw(splits[3], (TOKENS, D), 1.0, 6.0, ((0, 32),))
    norm_gains = jnp.clip(1.0 + 0.1 * jax.random.normal(splits[4], (2, D), jnp.float32), 0.5, 1.5)
    gains_moment = bell_draw(splits[5], (2, D), 30.0, 192.0, ((1, 16),), jnp.float32)
    gains_square = jnp.clip(jnp.exp(math.log(4000.0) - 1.609438 * jax.random.uniform(splits[6], (2, D), jnp.float32) ** level_of(splits[6], (2, D), ((1, 16),), -0.2, 0.2)), 800.0, 4000.0)
    w_qkv = draw_w_qkv(jax.random.fold_in(splits[22], 71), 0)
    qkv_moment = bell_draw(splits[8], (D, QKV), 20.0, 128.0, ((0, 16),), jnp.float32)
    qkv_square = jnp.clip(jnp.exp(math.log(1700.0) - 1.609438 * jax.random.uniform(splits[9], (D, QKV), jnp.float32) ** level_of(splits[9], (D, QKV), ((0, 16),), -0.2, 0.2)), 340.0, 1700.0)
    w_out = bell_draw(splits[10], (HQ * HD, D), (HQ * HD // 64) ** -0.5, 1.5, ((0, 16),), jnp.float32)
    out_moment = bell_draw(splits[11], (HQ * HD, D), 5.0, 32.0, ((0, 16),), jnp.float32)
    out_square = jnp.clip(jnp.exp(math.log(130.0) - 1.609438 * jax.random.uniform(splits[12], (HQ * HD, D), jnp.float32) ** level_of(splits[12], (HQ * HD, D), ((0, 16),), -0.2, 0.2)), 26.0, 130.0)
    w_router = draw_w_router(jax.random.fold_in(splits[22], 71), 0)
    router_moment = bell_draw(splits[14], (D, EXPERTS), 150.0, 896.0, ((0, 16),), jnp.float32)
    router_square = jnp.clip(jnp.exp(math.log(100000.0) - 1.609438 * jax.random.uniform(splits[15], (D, EXPERTS), jnp.float32) ** level_of(splits[15], (D, EXPERTS), ((0, 16),), -0.2, 0.2)), 20000.0, 100000.0)
    w_gate_up = bell_draw(splits[16], (EXPERTS, D, 2 * FF), D ** -0.5, 0.1875, ((0, 16), (1, 2)), jnp.float32)
    gate_up_moment = bell_draw(splits[17], (EXPERTS, D, 2 * FF), 7.0, 40.0, ((0, 16), (1, 2)), jnp.float32)
    gate_up_square = jnp.clip(jnp.exp(math.log(200.0) - 1.609438 * jax.random.uniform(splits[18], (EXPERTS, D, 2 * FF), jnp.float32) ** level_of(splits[18], (EXPERTS, D, 2 * FF), ((0, 16), (1, 2)), -0.2, 0.2)), 40.0, 200.0)
    w_down = bell_draw(splits[19], (EXPERTS, FF, D), (FF // 16) ** -0.5, 1.0, ((0, 16), (1, 2)), jnp.float32)
    down_moment = bell_draw(splits[20], (EXPERTS, FF, D), 1.0, 6.0, ((0, 16), (1, 2)), jnp.float32)
    down_square = jnp.clip(jnp.exp(math.log(5.0) - 1.609438 * jax.random.uniform(splits[21], (EXPERTS, FF, D), jnp.float32) ** level_of(splits[21], (EXPERTS, FF, D), ((0, 16), (1, 2)), -0.2, 0.2)), 1.0, 5.0)
    return {"hidden_in": hidden_in, "segments": segments, "routes": routes, "cotangent": cotangent, "norm_gains": norm_gains, "gains_moment": gains_moment, "gains_square": gains_square, "w_qkv": w_qkv, "qkv_moment": qkv_moment, "qkv_square": qkv_square, "w_out": w_out, "out_moment": out_moment, "out_square": out_square, "w_router": w_router, "router_moment": router_moment, "router_square": router_square, "w_gate_up": w_gate_up, "gate_up_moment": gate_up_moment, "gate_up_square": gate_up_square, "w_down": w_down, "down_moment": down_moment, "down_square": down_square}


eps_norm = 1e-06
rope_base = 10000.0
score_scale = 0.125
beta_one = 0.9
beta_two = 0.95
adam_eps = 1e-08
decay_matrix = 0.1
rate_gains = 0.2
rate_qkv = 0.01
rate_out = 0.05
rate_router = 0.01
rate_gate_up = 0.01
rate_down = 0.03
negative_big = -1e+30

def rounded(tensor):
    return lax.optimization_barrier(tensor.astype(jnp.bfloat16)).astype(jnp.float32)

def rms_forward(inputs, gain_vector):
    inv_rms = lax.rsqrt(lax.optimization_barrier(jnp.mean(inputs * inputs, axis=-1, keepdims=True)) + eps_norm)
    normed = inputs * inv_rms
    return (normed * gain_vector, normed, inv_rms)

def rms_backward(upstream, normed, inv_rms, gain_vector):
    gain_grad = lax.optimization_barrier(jnp.sum(upstream * normed, axis=0))
    scaled = upstream * gain_vector
    inner = lax.optimization_barrier(jnp.mean(scaled * normed, axis=-1, keepdims=True))
    return (inv_rms * (scaled - normed * inner), gain_grad)

def rotation_tables(positions, head_dim):
    half_dim = head_dim // 2
    frequency = rope_base ** (-2.0 * jnp.arange(half_dim, dtype=jnp.float32) / head_dim)
    angles = positions.astype(jnp.float32)[:, None] * frequency[None, :]
    return (jnp.cos(angles), jnp.sin(angles))

def rotate_heads(tensor, cosine, sine_table, direction_sign):
    half_dim = tensor.shape[-1] // 2
    first_half = tensor[..., :half_dim]
    second_half = tensor[..., half_dim:]
    cos_part = cosine[:, None, :]
    sin_part = sine_table[:, None, :] * direction_sign
    return jnp.concatenate([first_half * cos_part - second_half * sin_part, second_half * cos_part + first_half * sin_part], axis=-1)

def masked_scores(queries, key_rows, key_mask):
    scores = jnp.einsum('tkgd,skd->kgts', queries, key_rows) * score_scale
    return jnp.where(key_mask[None, None], scores, negative_big)

def attend_forward(queries, key_rows, value_rows, key_mask):
    scores = masked_scores(queries, key_rows, key_mask)
    row_max = lax.optimization_barrier(jnp.max(scores, axis=-1, keepdims=True))
    exp_total = lax.optimization_barrier(jnp.sum(jnp.exp(scores - row_max), axis=-1, keepdims=True))
    logsum = row_max + jnp.log(exp_total)
    probability = rounded(jnp.exp(scores - logsum))
    attended = jnp.einsum('kgts,skd->tkgd', probability, value_rows)
    return (attended.astype(jnp.bfloat16), logsum)

def attend_backward(queries, key_rows, value_rows, key_mask, logsum, attended, attended_grad):
    scores = masked_scores(queries, key_rows, key_mask)
    probability = jnp.exp(scores - logsum)
    row_delta = lax.optimization_barrier(jnp.sum(attended_grad * attended, axis=-1)).transpose(1, 2, 0)[..., None]
    value_grad = jnp.einsum('kgts,tkgd->skd', rounded(probability), attended_grad)
    prob_grad = jnp.einsum('tkgd,skd->kgts', attended_grad, value_rows)
    score_grad = rounded(probability * (prob_grad - row_delta) * score_scale)
    query_grad = jnp.einsum('kgts,skd->tkgd', score_grad, key_rows)
    key_grad = jnp.einsum('kgts,tkgd->skd', score_grad, queries)
    return (query_grad, key_grad, value_grad)

def adam_update(weight, moment, square, gradient, learn_rate, decay_value):
    new_moment = beta_one * moment + (1.0 - beta_one) * gradient
    new_square = beta_two * square + (1.0 - beta_two) * gradient * gradient
    corrected = new_moment / (1.0 - beta_one ** STEP)
    spread = new_square / (1.0 - beta_two ** STEP)
    new_weight = weight - learn_rate * (corrected / (jnp.sqrt(spread) + adam_eps) + decay_value * weight)
    return (new_weight, new_moment, new_square)

def reference(hidden_in, segments, routes, cotangent, norm_gains, gains_moment, gains_square, w_qkv, qkv_moment, qkv_square, w_out, out_moment, out_square, w_router, router_moment, router_square, w_gate_up, gate_up_moment, gate_up_square, w_down, down_moment, down_square):
    qkv_b = w_qkv.astype(jnp.bfloat16)
    out_b = w_out.astype(jnp.bfloat16)
    router_b = w_router.astype(jnp.bfloat16)
    gate_up_b = w_gate_up.astype(jnp.bfloat16)
    down_b = w_down.astype(jnp.bfloat16)
    gain_one = rounded(norm_gains[0])
    gain_two = rounded(norm_gains[1])
    group_size = HQ // HK
    q_cols = HQ * HD
    k_cols = HK * HD
    positions = jnp.arange(LENGTH, dtype=jnp.int32)
    cosine, sine_table = rotation_tables(positions, HD)
    causal = positions[None, :] <= positions[:, None]

    def project(seq_in, seg_row):
        inputs = seq_in.astype(jnp.float32)
        normed_one, plain_one, inv_one = rms_forward(inputs, gain_one)
        attend_in = normed_one.astype(jnp.bfloat16)
        projected = jnp.dot(attend_in, qkv_b, preferred_element_type=jnp.float32)
        queries = rounded(rotate_heads(projected[:, :q_cols].reshape(LENGTH, HQ, HD), cosine, sine_table, 1.0)).reshape(LENGTH, HK, group_size, HD)
        key_rows = rounded(rotate_heads(projected[:, q_cols:q_cols + k_cols].reshape(LENGTH, HK, HD), cosine, sine_table, 1.0))
        value_rows = rounded(projected[:, q_cols + k_cols:]).reshape(LENGTH, HK, HD)
        key_mask = (seg_row[None, :] == seg_row[:, None]) & causal
        return (inputs, plain_one, inv_one, attend_in, queries, key_rows, value_rows, key_mask)

    def attention_forward(pieces):
        seq_in, seg_row = pieces
        inputs, plain_one, inv_one, attend_in, queries, key_rows, value_rows, key_mask = project(seq_in, seg_row)
        attended, logsum = attend_forward(queries, key_rows, value_rows, key_mask)
        attended_flat = attended.reshape(LENGTH, q_cols)
        residual = inputs + jnp.dot(attended_flat, out_b, preferred_element_type=jnp.float32)
        return (residual, attended_flat, logsum)
    residual, attended_all, logsums = lax.map(attention_forward, (hidden_in.reshape(SEQS, LENGTH, D), segments))
    residual = residual.reshape(TOKENS, D)
    normed_two, plain_two, inv_two = rms_forward(residual, gain_two)
    moe_in = normed_two.astype(jnp.bfloat16)
    logits = jnp.dot(moe_in, router_b, preferred_element_type=jnp.float32)
    route_hot = routes[:, :, None] == jnp.arange(EXPERTS, dtype=jnp.int32)[None, None, :]
    chosen = lax.optimization_barrier(jnp.sum(jnp.where(route_hot, logits[:, None, :], 0.0), axis=-1))
    gate_weights = jax.nn.softmax(chosen, axis=-1)
    blocks = TOKENS // TOK_DEV
    pair_block = TOK_DEV * TOP
    pair_total = TOKENS * TOP
    block_rows = blocks * CAP
    flat_route = routes.reshape(blocks, pair_block)
    pair_hot = (flat_route[:, :, None] == jnp.arange(EXPERTS, dtype=jnp.int32)[None, None, :]).astype(jnp.int32)
    before = jnp.cumsum(pair_hot, axis=1) - pair_hot
    slot_index = lax.optimization_barrier(jnp.sum(before * pair_hot, axis=2))
    target = flat_route * block_rows + jnp.arange(blocks, dtype=jnp.int32)[:, None] * CAP + slot_index
    pair_table = jnp.full((EXPERTS * block_rows,), pair_total, jnp.int32).at[target.reshape(-1)].set(jnp.arange(pair_total, dtype=jnp.int32))
    padded_in = jnp.concatenate([moe_in, jnp.zeros((1, D), jnp.bfloat16)], axis=0)
    padded_cot = jnp.concatenate([cotangent.astype(jnp.float32), jnp.zeros((1, D), jnp.float32)], axis=0)
    padded_gate = jnp.concatenate([gate_weights.reshape(-1), jnp.zeros((1,), jnp.float32)], axis=0)

    def expert_step(running, expert_index):
        moe_sum, input_sum, gate_sum = running
        pair_rows = lax.dynamic_slice_in_dim(pair_table, expert_index * block_rows, block_rows)
        token_rows = pair_rows // TOP
        rows_in = padded_in[token_rows]
        pair_gate = padded_gate[pair_rows]
        cot_rows = padded_cot[token_rows]
        grad_rows = (pair_gate[:, None] * cot_rows).astype(jnp.bfloat16)
        gate_up_e = lax.dynamic_index_in_dim(gate_up_b, expert_index, 0, keepdims=False)
        down_e = lax.dynamic_index_in_dim(down_b, expert_index, 0, keepdims=False)
        pre_act = jnp.dot(rows_in, gate_up_e, preferred_element_type=jnp.float32)
        gate_part = pre_act[:, :FF]
        up_part = pre_act[:, FF:]
        sigmoid_gate = jax.nn.sigmoid(gate_part)
        silu_gate = gate_part * sigmoid_gate
        hidden_b = (silu_gate * up_part).astype(jnp.bfloat16)
        produced = jnp.dot(hidden_b, down_e, preferred_element_type=jnp.float32).astype(jnp.bfloat16)
        produced_f = produced.astype(jnp.float32)
        moe_sum = moe_sum.at[token_rows].add(pair_gate[:, None] * produced_f)
        gate_sum = gate_sum.at[pair_rows].add(lax.optimization_barrier(jnp.sum(cot_rows * produced_f, axis=1)))
        hidden_grad = jnp.dot(grad_rows, down_e.T, preferred_element_type=jnp.float32)
        down_grad = jnp.dot(hidden_b.T, grad_rows, preferred_element_type=jnp.float32)
        gate_grad_part = hidden_grad * up_part * sigmoid_gate * (1.0 + gate_part * (1.0 - sigmoid_gate))
        up_grad_part = hidden_grad * silu_gate
        both_grad = jnp.concatenate([gate_grad_part, up_grad_part], axis=1).astype(jnp.bfloat16)
        gate_up_grad = jnp.dot(rows_in.T, both_grad, preferred_element_type=jnp.float32)
        back_rows = jnp.dot(both_grad, gate_up_e.T, preferred_element_type=jnp.float32).astype(jnp.bfloat16)
        input_sum = input_sum.at[token_rows].add(back_rows.astype(jnp.float32))
        return ((moe_sum, input_sum, gate_sum), (gate_up_grad, down_grad))
    initial = (jnp.zeros((TOKENS + 1, D), jnp.float32), jnp.zeros((TOKENS + 1, D), jnp.float32), jnp.zeros((pair_total + 1,), jnp.float32))
    (moe_sum, input_sum, gate_sum), (gate_up_grad, down_grad) = lax.scan(expert_step, initial, jnp.arange(EXPERTS, dtype=jnp.int32))
    block_out = (residual + moe_sum[:TOKENS]).astype(jnp.bfloat16)
    gate_grad = gate_sum[:pair_total].reshape(TOKENS, TOP)
    choice_grad = gate_weights * (gate_grad - lax.optimization_barrier(jnp.sum(gate_weights * gate_grad, axis=-1, keepdims=True)))
    logits_grad = lax.optimization_barrier(jnp.sum(jnp.where(route_hot, choice_grad[:, :, None], 0.0), axis=1)).astype(jnp.bfloat16)
    router_grad = jnp.dot(moe_in.T, logits_grad, preferred_element_type=jnp.float32)
    moe_grad = jnp.dot(logits_grad, router_b.T, preferred_element_type=jnp.float32) + input_sum[:TOKENS]
    normed_two_grad, gain_two_grad = rms_backward(moe_grad, plain_two, inv_two, gain_two)
    residual_grad = cotangent.astype(jnp.float32) + normed_two_grad

    def attention_backward(running, pieces):
        qkv_acc, out_acc, gain_acc = running
        seq_in, seg_row, res_grad, attended_flat, logsum = pieces
        inputs, plain_one, inv_one, attend_in, queries, key_rows, value_rows, key_mask = project(seq_in, seg_row)
        residual_b = res_grad.astype(jnp.bfloat16)
        out_acc = out_acc + jnp.dot(attended_flat.T, residual_b, preferred_element_type=jnp.float32)
        attended_grad = rounded(jnp.dot(residual_b, out_b.T, preferred_element_type=jnp.float32)).reshape(LENGTH, HK, group_size, HD)
        attended_f = attended_flat.astype(jnp.float32).reshape(LENGTH, HK, group_size, HD)
        query_grad, key_grad, value_grad = attend_backward(queries, key_rows, value_rows, key_mask, logsum, attended_f, attended_grad)
        proj_grad = jnp.concatenate([rotate_heads(query_grad.reshape(LENGTH, HQ, HD), cosine, sine_table, -1.0).reshape(LENGTH, q_cols), rotate_heads(key_grad, cosine, sine_table, -1.0).reshape(LENGTH, k_cols), value_grad.reshape(LENGTH, k_cols)], axis=1).astype(jnp.bfloat16)
        qkv_acc = qkv_acc + jnp.dot(attend_in.T, proj_grad, preferred_element_type=jnp.float32)
        normed_grad = jnp.dot(proj_grad, qkv_b.T, preferred_element_type=jnp.float32)
        inputs_grad, gain_grad = rms_backward(normed_grad, plain_one, inv_one, gain_one)
        return ((qkv_acc, out_acc, gain_acc + gain_grad), res_grad + inputs_grad)
    start_grads = (jnp.zeros((D, QKV), jnp.float32), jnp.zeros((HQ * HD, D), jnp.float32), jnp.zeros((D,), jnp.float32))
    (qkv_grad, out_grad, gain_one_grad), input_grad = lax.scan(attention_backward, start_grads, (hidden_in.reshape(SEQS, LENGTH, D), segments, residual_grad.reshape(SEQS, LENGTH, D), attended_all, logsums))
    input_grad = input_grad.reshape(TOKENS, D)
    gains_grad = jnp.stack([gain_one_grad, gain_two_grad])
    new_gains, new_gains_moment, new_gains_square = adam_update(norm_gains, gains_moment, gains_square, gains_grad, rate_gains, 0.0)
    new_qkv, new_qkv_moment, new_qkv_square = adam_update(w_qkv, qkv_moment, qkv_square, qkv_grad, rate_qkv, decay_matrix)
    new_out, new_out_moment, new_out_square = adam_update(w_out, out_moment, out_square, out_grad, rate_out, decay_matrix)
    new_router, new_router_moment, new_router_square = adam_update(w_router, router_moment, router_square, router_grad, rate_router, decay_matrix)
    new_gate_up, new_gate_up_moment, new_gate_up_square = adam_update(w_gate_up, gate_up_moment, gate_up_square, gate_up_grad, rate_gate_up, decay_matrix)
    new_down, new_down_moment, new_down_square = adam_update(w_down, down_moment, down_square, down_grad, rate_down, decay_matrix)
    return (block_out, input_grad, gains_grad, qkv_grad, out_grad, router_grad, gate_up_grad, down_grad, new_gains, new_gains_moment, new_gains_square, new_qkv, new_qkv_moment, new_qkv_square, new_out, new_out_moment, new_out_square, new_router, new_router_moment, new_router_square, new_gate_up, new_gate_up_moment, new_gate_up_square, new_down, new_down_moment, new_down_square)
```

```python
import functools

import jax
import jax.numpy as jnp
from jax import lax
from jax.experimental import pallas as pl
from jax.experimental.pallas import tpu as pltpu
from jax.sharding import PartitionSpec as P

HQ = 16
HK = 8
HD = 64
TOP = 8
STEP = 3


eps_norm = 1e-06
rope_base = 10000.0
score_scale = 0.125
beta_one = 0.9
beta_two = 0.95
adam_eps = 1e-08
decay_matrix = 0.1
rate_gains = 0.2
rate_qkv = 0.01
rate_out = 0.05
rate_router = 0.01
rate_gate_up = 0.01
rate_down = 0.03
negative_big = -1e30


def rms_forward(inputs, gain_vector):
    inv_rms = lax.rsqrt(jnp.mean(inputs * inputs, axis=-1, keepdims=True) + eps_norm)
    normed = inputs * inv_rms
    return (normed * gain_vector, normed, inv_rms)


def rms_backward(upstream, normed, inv_rms, gain_vector):
    gain_grad = jnp.sum(upstream * normed, axis=0)
    scaled = upstream * gain_vector
    inner = jnp.mean(scaled * normed, axis=-1, keepdims=True)
    return (inv_rms * (scaled - normed * inner), gain_grad)


def rotation_tables(positions, head_dim):
    half_dim = head_dim // 2
    frequency = rope_base ** (-2.0 * jnp.arange(half_dim, dtype=jnp.float32) / head_dim)
    angles = positions.astype(jnp.float32)[:, None] * frequency[None, :]
    return (jnp.cos(angles), jnp.sin(angles))


def rotate_heads(tensor, cosine, sine_table, direction_sign):
    half_dim = tensor.shape[-1] // 2
    first_half = tensor[..., :half_dim]
    second_half = tensor[..., half_dim:]
    cos_part = cosine[:, None, :]
    sin_part = sine_table[:, None, :] * direction_sign
    return jnp.concatenate(
        [
            first_half * cos_part - second_half * sin_part,
            second_half * cos_part + first_half * sin_part,
        ],
        axis=-1,
    )


def after(value, anchor):
    return lax.optimization_barrier((value, anchor))[0]


def hop(value, offset, axis_size):
    return lax.ppermute(value, "dp", [(i, i ^ offset) for i in range(axis_size)])


def join(pieces):
    return pieces[0] if len(pieces) == 1 else jnp.concatenate(pieces, axis=0)


def halves(size):
    high = size // 4
    return (range(high // 2), range(high // 2, high))


def block_order(size):
    return [4 * k + 2 * x + c for part in halves(size) for c in (0, 1) for x in (0, 1) for k in part]


def gather_halves(block, size, first=None):
    base = block if first is None else after(block, first)
    near, far = halves(size)
    far_pieces = [hop(base, 4 * k, size) for k in far]
    near_pieces = [base] + [hop(base, 4 * k, size) for k in near[1:]]
    beside = [hop(base, 2, size)]
    if len(near) > 1:
        beside.append(hop(join(near_pieces[1:]), 2, size))
    near_rows = join(near_pieces + beside)
    near_rows = join([near_rows, hop(near_rows, 1, size)])
    far_rows = join(far_pieces)
    far_rows = join([far_rows, hop(far_rows, 2, size)])
    return [near_rows, join([far_rows, hop(far_rows, 1, size)])], far_pieces[-1]


def gather_plain(block, size, first):
    base = after(block, first)
    near, far = halves(size)
    pieces = [base] + [hop(base, 4 * k, size) for k in range(1, size // 4)]
    rows = join(pieces)
    rows = jnp.stack([rows, hop(rows, 2, size)])
    rows = jnp.stack([rows, hop(rows, 1, size)])
    rows = rows.reshape((2, 2, 2, -1) + block.shape[1:])
    return [rows[:, :, part].reshape((-1,) + block.shape[1:]) for part in (0, 1)], pieces[-1]


def gather_small(block, size):
    far = jnp.stack([block] + [hop(block, 4 * k, size) for k in range(1, size // 4)])
    pair = jnp.stack([far, hop(far, 2, size)], axis=1)
    return jnp.stack([pair, hop(pair, 1, size)], axis=2).reshape((size,) + block.shape)


def halve(part, offset, size):
    half = part.shape[0] // 2
    moved = hop(part[half:], offset, size)
    return (part[:half].astype(jnp.float32) + moved.astype(jnp.float32)).astype(jnp.bfloat16)


def reduce_rows(part, which, size):
    part = halve(halve(part, 1, size), 2, size)
    offsets = halves(size)[which]
    rows = part.shape[0] // len(offsets)
    pieces = [part[i * rows : (i + 1) * rows] for i in range(len(offsets))]
    return [hop(p, 4 * k, size) if k else p for p, k in zip(pieces, offsets)]


def order_matrix(own, size, width):
    block = width // size
    place = jnp.asarray(block_order(size), jnp.int32) ^ own
    column = (place[:, None] * block + jnp.arange(block, dtype=jnp.int32)[None, :]).reshape(-1)
    return (jnp.arange(width, dtype=jnp.int32)[:, None] == column[None, :]).astype(jnp.bfloat16)


def total_of(parts):
    total = parts[0].astype(jnp.float32)
    for part in parts[1:]:
        total = total + part.astype(jnp.float32)
    return total


def spread_small(block, size):
    grid = block.reshape((size // 4, 2, 2) + block.shape[1:])
    grid = jnp.stack([grid[0]] + [hop(grid[k], 4 * k, size) for k in range(1, size // 4)])
    grid = jnp.stack([grid[:, 0], hop(grid[:, 1], 2, size)], axis=1)
    grid = jnp.stack([grid[:, :, 0], hop(grid[:, :, 1], 1, size)], axis=2)
    return grid.reshape(block.shape)


def gather_rows(blocks, side, sides):
    if sides != 2:
        return [lax.all_gather(block, "shard", axis=0, tiled=True) for block in blocks]
    moved = lax.ppermute(join(blocks), "shard", [(0, 1), (1, 0)])
    result, start = [], 0
    for block in blocks:
        other = moved[start : start + block.shape[0]]
        start += block.shape[0]
        result.append(
            jnp.where(
                side == 0,
                jnp.concatenate([block, other], axis=0),
                jnp.concatenate([other, block], axis=0),
            )
        )
    return result


def scatter_rows(wholes, side, sides):
    if sides != 2:
        return [
            lax.psum_scatter(
                whole.astype(jnp.bfloat16), "shard", scatter_dimension=0, tiled=True
            ).astype(jnp.float32)
            for whole in wholes
        ]
    sent, kept = [], []
    for whole in wholes:
        rows = whole.shape[0] // 2
        upper, lower = whole[:rows], whole[rows:]
        sent.append(jnp.where(side == 0, lower, upper).astype(jnp.bfloat16))
        kept.append(jnp.where(side == 0, upper, lower))
    moved = lax.ppermute(join(sent), "shard", [(0, 1), (1, 0)]).astype(jnp.float32)
    result, start = [], 0
    for piece in kept:
        result.append(piece + moved[start : start + piece.shape[0]])
        start += piece.shape[0]
    return result


def sum_sides(value, sides):
    if sides != 2:
        return lax.psum(value.astype(jnp.bfloat16), "shard").astype(jnp.float32)
    own = value.astype(jnp.bfloat16)
    other = lax.ppermute(own, "shard", [(0, 1), (1, 0)])
    return own.astype(jnp.float32) + other.astype(jnp.float32)


def masked_scores(queries, key_rows, key_mask):
    scores = (
        jnp.einsum("tkgd,skd->kgts", queries, key_rows, preferred_element_type=jnp.float32)
        * score_scale
    )
    return jnp.where(key_mask[None, None], scores, negative_big)


def attend_forward(queries, key_rows, value_rows, key_mask):
    scores = masked_scores(queries, key_rows, key_mask)
    row_max = jnp.max(scores, axis=-1, keepdims=True)
    exp_total = jnp.sum(jnp.exp(scores - row_max), axis=-1, keepdims=True)
    logsum = row_max + jnp.log(exp_total)
    probability = jnp.exp(scores - logsum).astype(jnp.bfloat16)
    attended = jnp.einsum(
        "kgts,skd->tkgd", probability, value_rows, preferred_element_type=jnp.float32
    )
    return (attended.astype(jnp.bfloat16), logsum)

def attend_backward(queries, key_rows, value_rows, key_mask, logsum, attended, attended_grad):
    scores = masked_scores(queries, key_rows, key_mask)
    probability = jnp.exp(scores - logsum)
    row_delta = jnp.sum(
        attended_grad.astype(jnp.float32) * attended.astype(jnp.float32), axis=-1
    ).transpose(1, 2, 0)[..., None]
    value_grad = jnp.einsum(
        "kgts,tkgd->skd",
        probability.astype(jnp.bfloat16),
        attended_grad,
        preferred_element_type=jnp.float32,
    )
    prob_grad = jnp.einsum(
        "tkgd,skd->kgts", attended_grad, value_rows, preferred_element_type=jnp.float32
    )
    score_grad = (probability * (prob_grad - row_delta) * score_scale).astype(jnp.bfloat16)
    query_grad = jnp.einsum(
        "kgts,skd->tkgd", score_grad, key_rows, preferred_element_type=jnp.float32
    )
    key_grad = jnp.einsum("kgts,tkgd->skd", score_grad, queries, preferred_element_type=jnp.float32)
    return (query_grad, key_grad, value_grad)


def gates_of(logits, routed):
    shifted = jnp.where(routed, logits, negative_big)
    top_value = jnp.max(shifted, axis=-1, keepdims=True)
    raised = jnp.where(routed, jnp.exp(shifted - top_value), 0.0)
    return raised / jnp.sum(raised, axis=-1, keepdims=True)


def expert_kernel(
    owner_ref, rows_ref, cot_ref, hot_ref, router_ref, gate_up_ref, down_ref, down_in, gate_up_in,
    out_ref, grade_ref, back_ref, down_sum, gate_up_sum,
):
    @pl.when(pl.program_id(0) == 0)
    def _():
        down_sum[...] = down_in[...]
        gate_up_sum[...] = gate_up_in[...]

    last, first = (((1,), (1,)), ((), ())), (((0,), (0,)), ((), ()))
    half_dim = down_ref.shape[0]
    rows = rows_ref[...]
    cot_rows = cot_ref[...].astype(jnp.float32)
    gates = gates_of(
        jnp.dot(rows, router_ref[...], preferred_element_type=jnp.float32), hot_ref[...] > 0
    )
    ids = lax.broadcasted_iota(jnp.int32, gates.shape, 1)
    gate = jnp.sum(jnp.where(ids == owner_ref[0], gates, 0.0), axis=1, keepdims=True)
    pre_act = jnp.dot(rows, gate_up_ref[...], preferred_element_type=jnp.float32)
    gate_part = pre_act[:, :half_dim]
    up_part = pre_act[:, half_dim:]
    sigmoid_gate = jax.nn.sigmoid(gate_part)
    hidden_b = (gate_part * sigmoid_gate * up_part).astype(jnp.bfloat16)
    produced = jnp.dot(hidden_b, down_ref[...], preferred_element_type=jnp.float32)
    produced = produced.astype(jnp.bfloat16).astype(jnp.float32)
    out_ref[...] = (gate * produced).astype(jnp.bfloat16)
    grade = jnp.sum(cot_rows * produced, axis=1, keepdims=True)
    grade_ref[...] = jnp.broadcast_to(grade, grade_ref.shape)
    pair_grad = (gate * cot_rows).astype(jnp.bfloat16)
    hidden_grad = lax.dot_general(
        pair_grad, down_ref[...], last, preferred_element_type=jnp.float32
    )
    both_grad = jnp.concatenate(
        [
            hidden_grad * up_part * sigmoid_gate * (1.0 + gate_part * (1.0 - sigmoid_gate)),
            hidden_grad * gate_part * sigmoid_gate,
        ],
        axis=1,
    ).astype(jnp.bfloat16)
    back_ref[...] = lax.dot_general(
        both_grad, gate_up_ref[...], last, preferred_element_type=jnp.float32
    ).astype(jnp.bfloat16)
    down_sum[...] += lax.dot_general(
        hidden_b, pair_grad, first, preferred_element_type=jnp.float32
    )
    gate_up_sum[...] += lax.dot_general(
        rows, both_grad, first, preferred_element_type=jnp.float32
    )


def expert_pass(owner, rows, cot_rows, hot_rows, router, gate_up, down, down_sum, gate_up_sum):
    count, width = rows.shape
    experts = router.shape[1]
    tile = min(256, count)

    def whole(array):
        return pl.BlockSpec(array.shape, lambda i: (0, 0))

    def strip(columns):
        return pl.BlockSpec((tile, columns), lambda i: (i, 0))

    inner = down.shape[0]
    return pl.pallas_call(
        expert_kernel,
        grid=(count // tile,),
        in_specs=[
            pl.BlockSpec(memory_space=pltpu.SMEM),
            strip(width),
            strip(width),
            strip(experts),
            whole(router),
            whole(gate_up),
            whole(down),
            whole(down_sum),
            whole(gate_up_sum),
        ],
        out_specs=[strip(width), strip(128), strip(width), whole(down_sum), whole(gate_up_sum)],
        out_shape=[
            jax.ShapeDtypeStruct((count, width), jnp.bfloat16),
            jax.ShapeDtypeStruct((count, 128), jnp.float32),
            jax.ShapeDtypeStruct((count, width), jnp.bfloat16),
            jax.ShapeDtypeStruct(down_sum.shape, jnp.float32),
            jax.ShapeDtypeStruct(gate_up_sum.shape, jnp.float32),
        ],
        compiler_params=pltpu.CompilerParams(vmem_limit_bytes=52 * 2**20),
        cost_estimate=pl.CostEstimate(
            flops=18 * count * width * inner,
            bytes_accessed=count * width * 8 + 6 * 4 * width * inner,
            transcendentals=count * inner,
        ),
        name="expert",
    )(owner, rows, cot_rows, hot_rows, router, gate_up, down, down_sum, gate_up_sum)


def adam_update(weight, moment, square, gradient, learn_rate, decay_value):
    new_moment = beta_one * moment + (1.0 - beta_one) * gradient
    new_square = beta_two * square + (1.0 - beta_two) * gradient * gradient
    corrected = new_moment / (1.0 - beta_one**STEP)
    spread = new_square / (1.0 - beta_two**STEP)
    new_weight = weight - learn_rate * (
        corrected / (jnp.sqrt(spread) + adam_eps) + decay_value * weight
    )
    return (new_weight, new_moment, new_square)


def local(
    size,
    sides,
    hidden_in,
    segments,
    routes,
    cotangent,
    norm_gains,
    gains_moment,
    gains_square,
    w_qkv,
    qkv_moment,
    qkv_square,
    w_out,
    out_moment,
    out_square,
    w_router,
    router_moment,
    router_square,
    w_gate_up,
    gate_up_moment,
    gate_up_square,
    w_down,
    down_moment,
    down_square,
):
    own = lax.axis_index("dp")
    side = lax.axis_index("shard")
    tokens = hidden_in.shape[0]
    model_width = hidden_in.shape[1]
    experts = w_router.shape[1]
    group_size = HQ // HK
    q_cols = HQ * HD
    k_cols = HK * HD
    high = size // 4
    expert_ids = jnp.arange(experts, dtype=jnp.int32)
    order = own ^ jnp.arange(size, dtype=jnp.int32)

    hot_here = jnp.any(routes[:, :, None] == expert_ids[None, None, :], axis=1)
    small_parts = [
        norm_gains.astype(jnp.bfloat16).reshape(-1),
        w_router.astype(jnp.bfloat16).reshape(-1),
        hot_here.astype(jnp.bfloat16).reshape(-1),
    ]
    small_sizes = [part.shape[0] for part in small_parts]
    spare = -sum(small_sizes) % 1024
    small_flat = jnp.concatenate(small_parts + [jnp.zeros((spare,), jnp.bfloat16)])
    small_all = gather_small(small_flat.reshape(-1, 128), size).reshape(size, -1)
    qkv_parts, qkv_mark = gather_halves(w_qkv.astype(jnp.bfloat16), size)
    seg_here = segments[0]
    seg_prev = [
        lax.ppermute(seg_here, "shard", [(i, i + j) for i in range(sides - j)])
        for j in range(1, sides)
    ]
    gate_up_all, down_all = gather_rows(
        [w_gate_up[0].astype(jnp.bfloat16), w_down[0].astype(jnp.bfloat16)], side, sides
    )
    out_parts, out_mark = gather_plain(w_out.astype(jnp.bfloat16), size, qkv_mark)
    cot_parts, _ = gather_plain(cotangent, size, out_mark)

    first, second = small_sizes[0], small_sizes[0] + small_sizes[1]
    gains_abs = jnp.take(small_all[:, :first], order, axis=0).reshape(size, 2, -1)
    gain_one = gains_abs[:, 0, :].reshape(-1).astype(jnp.float32)
    gain_two = gains_abs[:, 1, :].reshape(-1).astype(jnp.float32)
    router_all = jnp.take(small_all[:, first:second], order, axis=0).reshape(model_width, experts)
    hot_rel = small_all[:, second : second + small_sizes[2]].reshape(2, high // 2, 2, 2, tokens, experts)
    hot_parts = hot_rel.transpose(0, 3, 2, 1, 4, 5).reshape(2, 2 * high * tokens, experts)
    place_matrix = order_matrix(own, size, model_width)
    head_matrix = order_matrix(own, size, q_cols)

    positions = side * tokens + jnp.arange(tokens, dtype=jnp.int32)
    cosine, sine_table = rotation_tables(positions, HD)
    inputs = hidden_in.astype(jnp.float32)
    normed_one, plain_one, inv_one = rms_forward(inputs, gain_one)
    attend_rel = jnp.dot(
        normed_one.astype(jnp.bfloat16), place_matrix, preferred_element_type=jnp.float32
    ).astype(jnp.bfloat16)
    qkv_rel = join(qkv_parts)
    projected = jnp.dot(attend_rel, qkv_rel, preferred_element_type=jnp.float32)
    queries = (
        rotate_heads(projected[:, :q_cols].reshape(tokens, HQ, HD), cosine, sine_table, 1.0)
        .astype(jnp.bfloat16)
        .reshape(tokens, HK, group_size, HD)
    )
    key_local = (
        rotate_heads(
            projected[:, q_cols : q_cols + k_cols].reshape(tokens, HK, HD), cosine, sine_table, 1.0
        )
        .astype(jnp.bfloat16)
        .reshape(tokens, k_cols)
    )
    value_local = projected[:, q_cols + k_cols :].astype(jnp.bfloat16)
    pair_local = jnp.concatenate([key_local, value_local], axis=1)
    pairs_here = [pair_local] + [
        lax.ppermute(pair_local, "shard", [(i, i + j) for i in range(sides - j)])
        for j in range(1, sides)
    ]
    pairs_all = jnp.concatenate(pairs_here, axis=0)
    length = pairs_all.shape[0]
    key_rows = pairs_all[:, :k_cols].reshape(length, HK, HD)
    value_rows = pairs_all[:, k_cols:].reshape(length, HK, HD)
    places = jnp.arange(tokens, dtype=jnp.int32)
    masks = [(seg_here[None, :] == seg_here[:, None]) & (places[None, :] <= places[:, None])]
    for j in range(1, sides):
        masks.append((seg_prev[j - 1][None, :] == seg_here[:, None]) & (side >= j))
    key_mask = jnp.concatenate(masks, axis=1)
    attended, logsum = attend_forward(queries, key_rows, value_rows, key_mask)
    attended_rel = jnp.dot(
        attended.reshape(tokens, q_cols), head_matrix, preferred_element_type=jnp.float32
    ).astype(jnp.bfloat16)
    out_rel = join(out_parts)
    residual = inputs + jnp.dot(attended_rel, out_rel, preferred_element_type=jnp.float32)
    normed_two, plain_two, inv_two = rms_forward(residual, gain_two)
    moe_in = normed_two.astype(jnp.bfloat16)

    moe_parts, _ = gather_halves(moe_in, size)
    owner = own.astype(jnp.int32).reshape(1)
    down_local = jnp.zeros(down_all.shape, jnp.float32)
    gate_up_local = jnp.zeros(gate_up_all.shape, jnp.float32)
    expert_rows, back_terms, grades = [], [], []
    for part in (0, 1):
        produced, grade, back_rows, down_local, gate_up_local = expert_pass(
            owner, moe_parts[part], cot_parts[part], hot_parts[part], router_all, gate_up_all,
            down_all, down_local, gate_up_local,
        )
        back_terms += reduce_rows(back_rows, part, size)
        expert_rows.append(produced)
        grades.append(grade[:, 0])
    out_terms = []
    for part in (1, 0):
        out_terms += reduce_rows(after(expert_rows[part], back_terms[-1]), part, size)
    grade_all = jnp.stack(grades).reshape(2, 2, 2, high // 2, tokens).transpose(0, 3, 2, 1, 4)
    grade_back = spread_small(grade_all.reshape(size, 1, tokens), size)
    gate_up_grad, down_grad = scatter_rows([gate_up_local, down_local], side, sides)
    gate_up_grad, down_grad = gate_up_grad[None], down_grad[None]
    block_out = (residual + total_of(out_terms)).astype(jnp.bfloat16)
    gate_grad = jnp.take(grade_back.reshape(size, tokens), order, axis=0).T
    logits_here = jnp.dot(moe_in, router_all, preferred_element_type=jnp.float32)
    gates_here = gates_of(logits_here, hot_here)
    choice_grad = gates_here * (
        gate_grad - jnp.sum(gates_here * gate_grad, axis=-1, keepdims=True)
    )
    logits_grad = jnp.where(hot_here, choice_grad, 0.0).astype(jnp.bfloat16)
    router_local = jnp.dot(moe_in.T, logits_grad, preferred_element_type=jnp.float32)
    moe_grad = jnp.dot(
        logits_grad, router_all.T, preferred_element_type=jnp.float32
    ) + total_of(back_terms)
    normed_two_grad, gain_two_grad = rms_backward(moe_grad, plain_two, inv_two, gain_two)
    residual_grad = cotangent.astype(jnp.float32) + normed_two_grad
    residual_b = residual_grad.astype(jnp.bfloat16)

    attended_grad = jnp.einsum(
        "tp,fp->tf",
        jnp.einsum("td,fd->tf", residual_b, out_rel, preferred_element_type=jnp.float32).astype(
            jnp.bfloat16
        ),
        head_matrix,
        preferred_element_type=jnp.float32,
    )
    attended_grad = attended_grad.astype(jnp.bfloat16).reshape(tokens, HK, group_size, HD)
    out_local = jnp.einsum(
        "tf,td->fd", attended_rel, residual_b, preferred_element_type=jnp.float32
    ).astype(jnp.bfloat16)
    half = q_cols // 2
    out_sums = reduce_rows(out_local[:half], 0, size) + reduce_rows(out_local[half:], 1, size)
    query_grad, key_grad, value_grad = attend_backward(
        queries, key_rows, value_rows, key_mask, logsum, attended, attended_grad
    )
    pair_grads = jnp.concatenate(
        [key_grad.reshape(length, k_cols), value_grad.reshape(length, k_cols)], axis=1
    )
    pair_own = pair_grads[:tokens]
    for j in range(1, sides):
        pair_own = pair_own + lax.ppermute(
            pair_grads[j * tokens : (j + 1) * tokens].astype(jnp.bfloat16),
            "shard",
            [(i + j, i) for i in range(sides - j)],
        ).astype(jnp.float32)
    proj_grad = jnp.concatenate(
        [
            rotate_heads(query_grad.reshape(tokens, HQ, HD), cosine, sine_table, -1.0).reshape(
                tokens, q_cols
            ),
            rotate_heads(
                pair_own[:, :k_cols].reshape(tokens, HK, HD), cosine, sine_table, -1.0
            ).reshape(tokens, k_cols),
            pair_own[:, k_cols:],
        ],
        axis=1,
    ).astype(jnp.bfloat16)
    qkv_sums = []
    half = model_width // 2
    for part in (1, 0):
        qkv_local = jnp.einsum(
            "td,tf->df",
            attend_rel[:, part * half : (part + 1) * half],
            proj_grad,
            preferred_element_type=jnp.float32,
        ).astype(jnp.bfloat16)
        qkv_sums += reduce_rows(qkv_local, part, size)
    normed_grad = jnp.einsum("tf,df->td", proj_grad, qkv_rel, preferred_element_type=jnp.float32)
    normed_grad = jnp.einsum(
        "tp,dp->td",
        normed_grad,
        place_matrix.astype(jnp.float32),
        precision=lax.Precision.HIGHEST,
        preferred_element_type=jnp.float32,
    )
    inputs_grad, gain_one_grad = rms_backward(normed_grad, plain_one, inv_one, gain_one)
    input_grad = residual_grad + inputs_grad

    router_flat = router_local.reshape(size, -1)
    gains_flat = jnp.stack([gain_one_grad, gain_two_grad]).reshape(2, size, -1)
    gains_flat = gains_flat.transpose(1, 0, 2).reshape(size, -1)
    small_local = jnp.concatenate([router_flat, gains_flat], axis=1).astype(jnp.bfloat16)
    small_local = jnp.take(small_local, order, axis=0)
    small_sum = jnp.sum(spread_small(small_local, size).astype(jnp.float32), axis=0)
    small_sum = sum_sides(small_sum, sides)
    router_grad = small_sum[: router_flat.shape[1]].reshape(w_router.shape)
    gains_grad = small_sum[router_flat.shape[1] :].reshape(norm_gains.shape)
    wide_sum = jnp.concatenate([total_of(qkv_sums), total_of(out_sums)], axis=1)
    wide_sum = sum_sides(wide_sum, sides)
    qkv_grad = wide_sum[:, : w_qkv.shape[1]]
    out_grad = wide_sum[:, w_qkv.shape[1] :]
    new_gains, new_gains_moment, new_gains_square = adam_update(
        norm_gains, gains_moment, gains_square, gains_grad, rate_gains, 0.0
    )
    new_qkv, new_qkv_moment, new_qkv_square = adam_update(
        w_qkv, qkv_moment, qkv_square, qkv_grad, rate_qkv, decay_matrix
    )
    new_out, new_out_moment, new_out_square = adam_update(
        w_out, out_moment, out_square, out_grad, rate_out, decay_matrix
    )
    new_router, new_router_moment, new_router_square = adam_update(
        w_router, router_moment, router_square, router_grad, rate_router, decay_matrix
    )
    new_gate_up, new_gate_up_moment, new_gate_up_square = adam_update(
        w_gate_up, gate_up_moment, gate_up_square, gate_up_grad, rate_gate_up, decay_matrix
    )
    new_down, new_down_moment, new_down_square = adam_update(
        w_down, down_moment, down_square, down_grad, rate_down, decay_matrix
    )
    return (
        block_out,
        input_grad,
        gains_grad,
        qkv_grad,
        out_grad,
        router_grad,
        gate_up_grad,
        down_grad,
        new_gains,
        new_gains_moment,
        new_gains_square,
        new_qkv,
        new_qkv_moment,
        new_qkv_square,
        new_out,
        new_out_moment,
        new_out_square,
        new_router,
        new_router_moment,
        new_router_square,
        new_gate_up,
        new_gate_up_moment,
        new_gate_up_square,
        new_down,
        new_down_moment,
        new_down_square,
    )


def solution(mesh):
    return jax.shard_map(
        functools.partial(local, mesh.shape["dp"], mesh.shape["shard"]),
        mesh=mesh,
        in_specs=(
            P(("dp", "shard"), None),
            P("dp", "shard"),
            P(("dp", "shard"), None),
            P(("dp", "shard"), None),
            P(None, "dp"),
            P(None, "dp"),
            P(None, "dp"),
            P("dp", None),
            P("dp", None),
            P("dp", None),
            P("dp", None),
            P("dp", None),
            P("dp", None),
            P("dp", None),
            P("dp", None),
            P("dp", None),
            P("dp", "shard", None),
            P("dp", "shard", None),
            P("dp", "shard", None),
            P("dp", "shard", None),
            P("dp", "shard", None),
            P("dp", "shard", None),
        ),
        out_specs=(
            P(("dp", "shard"), None),
            P(("dp", "shard"), None),
            P(None, "dp"),
            P("dp", None),
            P("dp", None),
            P("dp", None),
            P("dp", "shard", None),
            P("dp", "shard", None),
            P(None, "dp"),
            P(None, "dp"),
            P(None, "dp"),
            P("dp", None),
            P("dp", None),
            P("dp", None),
            P("dp", None),
            P("dp", None),
            P("dp", None),
            P("dp", None),
            P("dp", None),
            P("dp", None),
            P("dp", "shard", None),
            P("dp", "shard", None),
            P("dp", "shard", None),
            P("dp", "shard", None),
            P("dp", "shard", None),
            P("dp", "shard", None),
        ),
        check_vma=False,
    )
```

```python
import functools

import jax
import jax.numpy as jnp
from jax import lax
from jax.experimental import pallas as pl
from jax.experimental.pallas import tpu as pltpu
from jax.sharding import PartitionSpec as P


HQ = 16
HK = 8
HD = 64
STEP = 3


eps_norm = 1e-06
rope_base = 10000.0
score_scale = 0.125
beta_one = 0.9
beta_two = 0.95
adam_eps = 1e-08
decay_matrix = 0.1
rate_gains = 0.2
rate_qkv = 0.01
rate_out = 0.05
rate_router = 0.01
rate_gate_up = 0.01
rate_down = 0.03
negative_big = -1e30


def rms_forward(inputs, gain_vector):
    inv_rms = lax.rsqrt(jnp.mean(inputs * inputs, axis=-1, keepdims=True) + eps_norm)
    normed = inputs * inv_rms
    return (normed * gain_vector, normed, inv_rms)


def rms_backward(upstream, normed, inv_rms, gain_vector):
    gain_grad = jnp.sum(upstream * normed, axis=0)
    scaled = upstream * gain_vector
    inner = jnp.mean(scaled * normed, axis=-1, keepdims=True)
    return (inv_rms * (scaled - normed * inner), gain_grad)


def rotation_tables(positions, head_dim):
    half_dim = head_dim // 2
    frequency = rope_base ** (-2.0 * jnp.arange(half_dim, dtype=jnp.float32) / head_dim)
    angles = positions.astype(jnp.float32)[:, None] * frequency[None, :]
    return (jnp.cos(angles), jnp.sin(angles))


def rotate_heads(tensor, cosine, sine_table, direction_sign):
    half_dim = tensor.shape[-1] // 2
    first_half = tensor[..., :half_dim]
    second_half = tensor[..., half_dim:]
    cos_part = cosine[:, None, :]
    sin_part = sine_table[:, None, :] * direction_sign
    return jnp.concatenate(
        [
            first_half * cos_part - second_half * sin_part,
            second_half * cos_part + first_half * sin_part,
        ],
        axis=-1,
    )


DP, SHARD = "dp", "shard"


def after(value, anchor):
    return lax.optimization_barrier((value, anchor))[0]


def hop(value, offset, axis_size):
    return lax.ppermute(value, DP, [(i, i ^ offset) for i in range(axis_size)])


def to_side(value, pairs):
    return lax.ppermute(value, SHARD, pairs)


def join(pieces):
    return pieces[0] if len(pieces) == 1 else jnp.concatenate(pieces, axis=0)


def halves(size):
    high = size // 4
    return (range(high // 2), range(high // 2, high))


def block_order(size):
    return [4 * k + 2 * x + c for part in halves(size) for c in (0, 1) for x in (0, 1) for k in part]


def plain_order(size):
    return [4 * k + 2 * x + c for c in (0, 1) for x in (0, 1) for k in range(size // 4)]


def gather_halves(block, size):
    near, far = halves(size)
    near_pieces = [block] + [hop(block, 4 * k, size) for k in near[1:]]
    far_pieces = [hop(block, 4 * k, size) for k in far]
    beside = [hop(block, 2, size)]
    if len(near) > 1:
        beside.append(hop(join(near_pieces[1:]), 2, size))
    near_rows = join(near_pieces + beside)
    near_rows = [near_rows, hop(near_rows, 1, size)]
    far_rows = join(far_pieces)
    far_rows = join([far_rows, hop(far_rows, 2, size)])
    return [near_rows, [far_rows, hop(far_rows, 1, size)]]


def gather_plain(block, size):
    pieces = [block] + [hop(block, 4 * k, size) for k in range(1, size // 4)]
    rows = join(pieces)
    rows = jnp.stack([rows, hop(rows, 2, size)])
    rows = rows.reshape((-1,) + block.shape[1:])
    return [rows, hop(rows, 1, size)]


def gather_small(block, size):
    far = [hop(block, 4 * k, size) for k in range(1, size // 4)]
    far = jnp.stack([block] + far)
    pair = jnp.stack([far, hop(far, 2, size)], axis=1)
    return jnp.stack([pair, hop(pair, 1, size)], axis=2).reshape((size,) + block.shape)


def halve(part, offset, size):
    half = part.shape[0] // 2
    moved = hop(part[half:], offset, size)
    return (part[:half].astype(jnp.float32) + moved.astype(jnp.float32)).astype(jnp.bfloat16)


def reduce_rows(part, offsets, size):
    return send_rows(halve(part, 1, size), offsets, size)


def send_rows(part, offsets, size):
    part = halve(part, 2, size)
    rows = part.shape[0] // len(offsets)
    pieces = [part[i * rows : (i + 1) * rows] for i in range(len(offsets))]
    terms = [hop(p, 4 * k, size) if k else p for p, k in zip(pieces, offsets)]
    return terms, part


def order_matrix(own, size, width, offsets):
    block = width // size
    place = jnp.asarray(offsets, jnp.int32) ^ own
    column = (place[:, None] * block + jnp.arange(block, dtype=jnp.int32)[None, :]).reshape(-1)
    return (jnp.arange(width, dtype=jnp.int32)[:, None] == column[None, :]).astype(jnp.bfloat16)


def total_of(parts):
    total = parts[0].astype(jnp.float32)
    for part in parts[1:]:
        total = total + part.astype(jnp.float32)
    return total


def spread_small(block, size):
    grid = block.reshape((size // 4, 2, 2) + block.shape[1:])
    grid = jnp.stack([grid[:, :, 0], hop(grid[:, :, 1], 1, size)], axis=2)
    grid = jnp.stack([grid[:, 0], hop(grid[:, 1], 2, size)], axis=1)
    far = [hop(grid[k], 4 * k, size) for k in range(1, size // 4)]
    grid = jnp.stack([grid[0]] + far)
    return grid.reshape(block.shape)


def gather_weights(blocks, side, sides):
    if sides != 2:
        return [lax.all_gather(block, SHARD, axis=0, tiled=True) for block in blocks]
    joined = join(blocks)
    moved = to_side(joined, [(0, 1), (1, 0)])
    return [joined, moved, side.astype(jnp.int32).reshape(1)]


def scatter_rows(wholes, side, sides):
    if sides != 2:
        summed = [
            lax.psum_scatter(
                whole.astype(jnp.bfloat16), SHARD, scatter_dimension=0, tiled=True
            ).astype(jnp.float32)
            for whole in wholes
        ]
        return summed, None
    sent, kept = [], []
    for whole in wholes:
        rows = whole.shape[0] // 2
        upper, lower = whole[:rows], whole[rows:]
        sent.append(jnp.where(side == 0, lower, upper).astype(jnp.bfloat16))
        kept.append(jnp.where(side == 0, upper, lower))
    moved = to_side(join(sent), [(0, 1), (1, 0)])
    return kept, moved


def add_moved(kept, moved):
    result, start = [], 0
    for piece in kept:
        result.append(piece + moved[start : start + piece.shape[0]].astype(jnp.float32))
        start += piece.shape[0]
    return result


def sum_sides(value, sides):
    if sides != 2:
        return lax.psum(value.astype(jnp.bfloat16), SHARD).astype(jnp.float32)
    own = value.astype(jnp.bfloat16)
    other = to_side(own, [(0, 1), (1, 0)])
    return own.astype(jnp.float32) + other.astype(jnp.float32)


def masked_scores(queries, key_rows, key_mask):
    scores = (
        jnp.einsum("tkgd,skd->kgts", queries, key_rows, preferred_element_type=jnp.float32)
        * score_scale
    )
    return jnp.where(key_mask[None, None], scores, negative_big)


def attend_forward(queries, key_rows, value_rows, key_mask):
    scores = masked_scores(queries, key_rows, key_mask)
    row_max = jnp.max(scores, axis=-1, keepdims=True)
    exp_total = jnp.sum(jnp.exp(scores - row_max), axis=-1, keepdims=True)
    logsum = row_max + jnp.log(exp_total)
    probability = jnp.exp(scores - logsum).astype(jnp.bfloat16)
    attended = jnp.einsum(
        "kgts,skd->tkgd", probability, value_rows, preferred_element_type=jnp.float32
    )
    return (attended.astype(jnp.bfloat16), logsum)


def attend_backward(queries, key_rows, value_rows, key_mask, logsum, attended, attended_grad):
    scores = masked_scores(queries, key_rows, key_mask)
    probability = jnp.exp(scores - logsum)
    row_delta = jnp.sum(
        attended_grad.astype(jnp.float32) * attended.astype(jnp.float32), axis=-1
    ).transpose(1, 2, 0)[..., None]
    value_grad = jnp.einsum(
        "kgts,tkgd->skd",
        probability.astype(jnp.bfloat16),
        attended_grad,
        preferred_element_type=jnp.float32,
    )
    prob_grad = jnp.einsum(
        "tkgd,skd->kgts", attended_grad, value_rows, preferred_element_type=jnp.float32
    )
    score_grad = (probability * (prob_grad - row_delta) * score_scale).astype(jnp.bfloat16)
    query_grad = jnp.einsum(
        "kgts,skd->tkgd", score_grad, key_rows, preferred_element_type=jnp.float32
    )
    key_grad = jnp.einsum("kgts,tkgd->skd", score_grad, queries, preferred_element_type=jnp.float32)
    return (query_grad, key_grad, value_grad)


def gates_of(logits, routed):
    shifted = jnp.where(routed, logits, negative_big)
    top_value = jnp.max(shifted, axis=-1, keepdims=True)
    raised = jnp.where(routed, jnp.exp(shifted - top_value), 0.0)
    return raised / jnp.sum(raised, axis=-1, keepdims=True)


def expert_kernel(
    weight_count, sum_count,
    owner_ref, rows_ref, rows_other, cot_ref, cot_other, hot_ref, router_ref, *more_refs
):
    weight_refs, more_refs = more_refs[:weight_count], more_refs[weight_count:]
    sums_in, more_refs = more_refs[:sum_count], more_refs[sum_count:]
    out_ref, grade_ref, back_ref, down_sum, gate_up_sum, *scratch = more_refs
    gate_up_ref, down_ref = scratch if scratch else weight_refs

    @pl.when(pl.program_id(0) == 0)
    def _():
        if sums_in:
            down_sum[...] = sums_in[0][...]
            gate_up_sum[...] = sums_in[1][...]
        else:
            down_sum[...] = jnp.zeros_like(down_sum)
            gate_up_sum[...] = jnp.zeros_like(gate_up_sum)
        if scratch:
            place = weight_refs[2][0]
            upper = gate_up_ref.shape[0] // 2
            lower = down_ref.shape[0] // 2
            for source, where in ((weight_refs[0], place), (weight_refs[1], 1 - place)):
                gate_up_ref[pl.ds(pl.multiple_of(where * upper, upper), upper), :] = source[:upper]
                down_ref[pl.ds(pl.multiple_of(where * lower, lower), lower), :] = source[upper:]

    last, first = (((1,), (1,)), ((), ())), (((0,), (0,)), ((), ()))
    half_dim = down_ref.shape[0]
    mine = pl.program_id(0) < pl.num_programs(0) // 2
    rows = jnp.where(mine, rows_ref[...], rows_other[...])
    cot_rows = jnp.where(mine, cot_ref[...], cot_other[...]).astype(jnp.float32)
    gates = gates_of(
        jnp.dot(rows, router_ref[...], preferred_element_type=jnp.float32), hot_ref[...] > 0
    )
    ids = lax.broadcasted_iota(jnp.int32, gates.shape, 1)
    gate = jnp.sum(jnp.where(ids == owner_ref[0], gates, 0.0), axis=1, keepdims=True)
    pre_act = jnp.dot(rows, gate_up_ref[...], preferred_element_type=jnp.float32)
    gate_part = pre_act[:, :half_dim]
    up_part = pre_act[:, half_dim:]
    sigmoid_gate = jax.nn.sigmoid(gate_part)
    hidden_b = (gate_part * sigmoid_gate * up_part).astype(jnp.bfloat16)
    produced = jnp.dot(hidden_b, down_ref[...], preferred_element_type=jnp.float32)
    produced = produced.astype(jnp.bfloat16).astype(jnp.float32)
    out_ref[...] = (gate * produced).astype(jnp.bfloat16)
    grade = jnp.sum(cot_rows * produced, axis=1, keepdims=True)
    grade_ref[...] = jnp.broadcast_to(grade, grade_ref.shape)
    pair_grad = (gate * cot_rows).astype(jnp.bfloat16)
    hidden_grad = lax.dot_general(
        pair_grad, down_ref[...], last, preferred_element_type=jnp.float32
    )
    both_grad = jnp.concatenate(
        [
            hidden_grad * up_part * sigmoid_gate * (1.0 + gate_part * (1.0 - sigmoid_gate)),
            hidden_grad * gate_part * sigmoid_gate,
        ],
        axis=1,
    ).astype(jnp.bfloat16)
    back_ref[...] = lax.dot_general(
        both_grad, gate_up_ref[...], last, preferred_element_type=jnp.float32
    ).astype(jnp.bfloat16)
    down_sum[...] += lax.dot_general(
        hidden_b, pair_grad, first, preferred_element_type=jnp.float32
    )
    gate_up_sum[...] += lax.dot_general(
        rows, both_grad, first, preferred_element_type=jnp.float32
    )


def expert_pass(owner, rows, cot_parts, part, hot_rows, router, weights, sums):
    count, width = 2 * rows[0].shape[0], rows[0].shape[1]
    experts = router.shape[1]
    tile = min(256, count // 4)
    run = count // 4 // tile

    def cot_place(i):
        return i // run * 2 * run + part * run + i % run

    def whole(array):
        return pl.BlockSpec(array.shape, lambda i: (0, 0))

    def strip(columns):
        return pl.BlockSpec((tile, columns), lambda i: (i, 0))

    if len(weights) == 3:
        inner = 2 * (weights[0].shape[0] - width // 2)
        weight_specs = [whole(weights[0]), whole(weights[1]), pl.BlockSpec(memory_space=pltpu.SMEM)]
        scratch = [
            pltpu.VMEM((width, 2 * inner), jnp.bfloat16),
            pltpu.VMEM((inner, width), jnp.bfloat16),
        ]
    else:
        inner = weights[1].shape[0]
        weight_specs, scratch = [whole(array) for array in weights], []
    down = jax.ShapeDtypeStruct((inner, width), jnp.float32)
    gate_up = jax.ShapeDtypeStruct((width, 2 * inner), jnp.float32)
    return pl.pallas_call(
        functools.partial(expert_kernel, len(weights), len(sums)),
        grid=(count // tile,),
        in_specs=[
            pl.BlockSpec(memory_space=pltpu.SMEM),
            pl.BlockSpec((tile, width), lambda i: (jnp.minimum(i, 2 * run - 1), 0)),
            pl.BlockSpec((tile, width), lambda i: (jnp.maximum(i - 2 * run, 0), 0)),
            pl.BlockSpec((tile, width), lambda i: (cot_place(jnp.minimum(i, 2 * run - 1)), 0)),
            pl.BlockSpec((tile, width), lambda i: (cot_place(jnp.maximum(i - 2 * run, 0)), 0)),
            strip(experts),
            whole(router),
        ]
        + weight_specs
        + [whole(array) for array in sums],
        out_specs=[strip(width), strip(128), strip(width), whole(down), whole(gate_up)],
        out_shape=[
            jax.ShapeDtypeStruct((count, width), jnp.bfloat16),
            jax.ShapeDtypeStruct((count, 128), jnp.float32),
            jax.ShapeDtypeStruct((count, width), jnp.bfloat16),
            down,
            gate_up,
        ],
        scratch_shapes=scratch,
        compiler_params=pltpu.CompilerParams(vmem_limit_bytes=52 * 2**20),
        cost_estimate=pl.CostEstimate(
            flops=18 * count * width * inner,
            bytes_accessed=count * width * 8 + 6 * 4 * width * inner,
            transcendentals=count * inner,
        ),
        name="expert",
    )(owner, *rows, *cot_parts, hot_rows, router, *weights, *sums)


def adam_update(weight, moment, square, gradient, learn_rate, decay_value):
    new_moment = beta_one * moment + (1.0 - beta_one) * gradient
    new_square = beta_two * square + (1.0 - beta_two) * gradient * gradient
    corrected = new_moment / (1.0 - beta_one**STEP)
    spread = new_square / (1.0 - beta_two**STEP)
    new_weight = weight - learn_rate * (
        corrected / (jnp.sqrt(spread) + adam_eps) + decay_value * weight
    )
    return (new_weight, new_moment, new_square)


def local(
    size,
    sides,
    hidden_in,
    segments,
    routes,
    cotangent,
    norm_gains,
    gains_moment,
    gains_square,
    w_qkv,
    qkv_moment,
    qkv_square,
    w_out,
    out_moment,
    out_square,
    w_router,
    router_moment,
    router_square,
    w_gate_up,
    gate_up_moment,
    gate_up_square,
    w_down,
    down_moment,
    down_square,
):
    own = lax.axis_index(DP)
    side = lax.axis_index(SHARD)
    tokens = hidden_in.shape[0]
    model_width = hidden_in.shape[1]
    experts = w_router.shape[1]
    group_size = HQ // HK
    q_cols = HQ * HD
    k_cols = HK * HD
    high = size // 4
    expert_ids = jnp.arange(experts, dtype=jnp.int32)
    order = own ^ jnp.arange(size, dtype=jnp.int32)

    hot_here = jnp.any(routes[:, :, None] == expert_ids[None, None, :], axis=1)
    small_parts = [
        norm_gains.astype(jnp.bfloat16).reshape(-1),
        w_router.astype(jnp.bfloat16).reshape(-1),
        hot_here.astype(jnp.bfloat16).reshape(-1),
    ]
    small_sizes = [part.shape[0] for part in small_parts]
    spare = -sum(small_sizes) % 1024
    small_flat = jnp.concatenate(small_parts + [jnp.zeros((spare,), jnp.bfloat16)])
    small_all = gather_small(small_flat.reshape(-1, 128), size).reshape(size, -1)
    qkv_parts = gather_halves(w_qkv.astype(jnp.bfloat16), size)
    seg_here = segments[0]
    seg_prev = [to_side(seg_here, [(i, i + j) for i in range(sides - j)]) for j in range(1, sides)]
    weights = gather_weights(
        [w_gate_up[0].astype(jnp.bfloat16), w_down[0].astype(jnp.bfloat16)], side, sides
    )
    out_parts = gather_plain(w_out.astype(jnp.bfloat16), size)
    cot_parts = gather_plain(cotangent, size)

    first, second = small_sizes[0], small_sizes[0] + small_sizes[1]
    gains_abs = jnp.take(small_all[:, :first], order, axis=0).reshape(size, 2, -1)
    gain_one = gains_abs[:, 0, :].reshape(-1).astype(jnp.float32)
    gain_two = gains_abs[:, 1, :].reshape(-1).astype(jnp.float32)
    router_all = jnp.take(small_all[:, first:second], order, axis=0).reshape(model_width, experts)
    hot_rel = small_all[:, second : second + small_sizes[2]].reshape(2, high // 2, 2, 2, tokens, experts)
    hot_parts = hot_rel.transpose(0, 3, 2, 1, 4, 5).reshape(2, 2 * high * tokens, experts)
    place_matrix = order_matrix(own, size, model_width, block_order(size))
    head_matrix = order_matrix(own, size, q_cols, plain_order(size))

    positions = side * tokens + jnp.arange(tokens, dtype=jnp.int32)
    cosine, sine_table = rotation_tables(positions, HD)
    inputs = hidden_in.astype(jnp.float32)
    normed_one, plain_one, inv_one = rms_forward(inputs, gain_one)
    attend_rel = jnp.dot(
        normed_one.astype(jnp.bfloat16), place_matrix, preferred_element_type=jnp.float32
    ).astype(jnp.bfloat16)
    qkv_rel = join(qkv_parts[0] + qkv_parts[1])
    out_rel = join(out_parts)
    projected = jnp.dot(attend_rel, qkv_rel, preferred_element_type=jnp.float32)
    queries = (
        rotate_heads(projected[:, :q_cols].reshape(tokens, HQ, HD), cosine, sine_table, 1.0)
        .astype(jnp.bfloat16)
        .reshape(tokens, HK, group_size, HD)
    )
    key_local = (
        rotate_heads(
            projected[:, q_cols : q_cols + k_cols].reshape(tokens, HK, HD), cosine, sine_table, 1.0
        )
        .astype(jnp.bfloat16)
        .reshape(tokens, k_cols)
    )
    value_local = projected[:, q_cols + k_cols :].astype(jnp.bfloat16)
    pair_local = jnp.concatenate([key_local, value_local], axis=1)
    pairs_here = [pair_local] + [
        to_side(pair_local, [(i, i + j) for i in range(sides - j)])
        for j in range(1, sides)
    ]
    pairs_all = jnp.concatenate(pairs_here, axis=0)
    length = pairs_all.shape[0]
    key_rows = pairs_all[:, :k_cols].reshape(length, HK, HD)
    value_rows = pairs_all[:, k_cols:].reshape(length, HK, HD)
    places = jnp.arange(tokens, dtype=jnp.int32)
    masks = [(seg_here[None, :] == seg_here[:, None]) & (places[None, :] <= places[:, None])]
    for j in range(1, sides):
        masks.append((seg_prev[j - 1][None, :] == seg_here[:, None]) & (side >= j))
    key_mask = jnp.concatenate(masks, axis=1)
    attended, logsum = attend_forward(queries, key_rows, value_rows, key_mask)
    attended_rel = jnp.dot(
        attended.reshape(tokens, q_cols), head_matrix, preferred_element_type=jnp.float32
    ).astype(jnp.bfloat16)
    mixed = jnp.dot(attended_rel, out_rel, preferred_element_type=jnp.float32)
    residual = inputs + mixed
    normed_two, plain_two, inv_two = rms_forward(residual, gain_two)
    moe_in = normed_two.astype(jnp.bfloat16)

    moe_parts = gather_halves(moe_in, size)
    owner = own.astype(jnp.int32).reshape(1)
    sums, back_halves, expert_rows, grades = [], [], [], []
    for part in (0, 1):
        produced, grade, back_rows, *sums = expert_pass(
            owner, moe_parts[part], cot_parts, part, hot_parts[part], router_all, weights, sums
        )
        back_halves.append(halve(back_rows, 1, size))
        expert_rows.append(produced)
        grades.append(grade[:, 0])
    back_far, back_mark = send_rows(back_halves[1], halves(size)[1], size)
    back_near, _ = send_rows(after(back_halves[0], back_mark), halves(size)[0], size)
    back_terms = back_near + back_far
    back_total = total_of(back_terms)
    out_terms = reduce_rows(expert_rows[0], halves(size)[0], size)[0]
    out_terms += reduce_rows(expert_rows[1], halves(size)[1], size)[0]
    grade_all = jnp.stack(grades).reshape(2, 2, 2, high // 2, tokens).transpose(0, 3, 2, 1, 4)
    grade_back = spread_small(grade_all.reshape(size, 1, tokens), size)
    down_local, gate_up_local = sums
    gate_up_local, down_local, _ = lax.optimization_barrier(
        (gate_up_local, down_local, back_halves[1])
    )
    kept, moved = scatter_rows([gate_up_local, down_local], side, sides)
    gate_grad = jnp.take(grade_back.reshape(size, tokens), order, axis=0).T
    logits_here = jnp.dot(moe_in, router_all, preferred_element_type=jnp.float32)
    gates_here = gates_of(logits_here, hot_here)
    choice_grad = gates_here * (
        gate_grad - jnp.sum(gates_here * gate_grad, axis=-1, keepdims=True)
    )
    logits_grad = jnp.where(hot_here, choice_grad, 0.0).astype(jnp.bfloat16)
    router_local = jnp.dot(moe_in.T, logits_grad, preferred_element_type=jnp.float32)
    moe_grad = jnp.dot(
        logits_grad, router_all.T, preferred_element_type=jnp.float32
    ) + back_total
    normed_two_grad, gain_two_grad = rms_backward(moe_grad, plain_two, inv_two, gain_two)
    residual_grad = cotangent.astype(jnp.float32) + normed_two_grad
    residual_b = residual_grad.astype(jnp.bfloat16)

    grad_rel = jnp.einsum("td,fd->tf", residual_b, out_rel, preferred_element_type=jnp.float32)
    attended_grad = jnp.einsum(
        "tp,fp->tf",
        grad_rel.astype(jnp.bfloat16),
        head_matrix,
        preferred_element_type=jnp.float32,
    )
    attended_grad = attended_grad.astype(jnp.bfloat16).reshape(tokens, HK, group_size, HD)
    out_local = jnp.einsum(
        "tf,td->fd", attended_rel, residual_b, preferred_element_type=jnp.float32
    ).astype(jnp.bfloat16)
    out_sums = reduce_rows(out_local, range(high), size)[0]
    query_grad, key_grad, value_grad = attend_backward(
        queries, key_rows, value_rows, key_mask, logsum, attended, attended_grad
    )
    pair_grads = jnp.concatenate(
        [key_grad.reshape(length, k_cols), value_grad.reshape(length, k_cols)], axis=1
    )
    pair_own = pair_grads[:tokens]
    for j in range(1, sides):
        pair_own = pair_own + to_side(
            pair_grads[j * tokens : (j + 1) * tokens].astype(jnp.bfloat16),
            [(i + j, i) for i in range(sides - j)],
        ).astype(jnp.float32)
    proj_grad = jnp.concatenate(
        [
            rotate_heads(query_grad.reshape(tokens, HQ, HD), cosine, sine_table, -1.0).reshape(
                tokens, q_cols
            ),
            rotate_heads(
                pair_own[:, :k_cols].reshape(tokens, HK, HD), cosine, sine_table, -1.0
            ).reshape(tokens, k_cols),
            pair_own[:, k_cols:],
        ],
        axis=1,
    ).astype(jnp.bfloat16)
    qkv_halves = []
    half = model_width // 2
    for part in (1, 0):
        qkv_local = jnp.einsum(
            "td,tf->df",
            attend_rel[:, part * half : (part + 1) * half],
            proj_grad,
            preferred_element_type=jnp.float32,
        ).astype(jnp.bfloat16)
        qkv_halves.append(halve(qkv_local, 1, size))
    qkv_far, qkv_mark = send_rows(qkv_halves[0], halves(size)[1], size)
    qkv_near, _ = send_rows(after(qkv_halves[1], qkv_mark), halves(size)[0], size)
    qkv_sums = qkv_near + qkv_far
    normed_grad = jnp.einsum("tf,df->td", proj_grad, qkv_rel, preferred_element_type=jnp.float32)
    normed_grad = jnp.einsum(
        "tp,dp->td",
        normed_grad,
        place_matrix.astype(jnp.float32),
        precision=lax.Precision.HIGHEST,
        preferred_element_type=jnp.float32,
    )
    inputs_grad, gain_one_grad = rms_backward(normed_grad, plain_one, inv_one, gain_one)
    input_grad = residual_grad + inputs_grad

    kept = [after(piece, qkv_mark) for piece in kept]
    if moved is not None:
        kept = add_moved(kept, moved)
    gate_up_grad, down_grad = kept[0][None], kept[1][None]
    block_out = (after(residual, qkv_mark) + total_of(out_terms)).astype(jnp.bfloat16)
    router_flat = router_local.reshape(size, -1)
    gains_flat = jnp.stack([gain_one_grad, gain_two_grad]).reshape(2, size, -1)
    gains_flat = gains_flat.transpose(1, 0, 2).reshape(size, -1)
    small_local = jnp.concatenate([router_flat, gains_flat], axis=1).astype(jnp.bfloat16)
    small_local = jnp.take(small_local, order, axis=0)
    small_sum = jnp.sum(spread_small(small_local, size).astype(jnp.float32), axis=0)
    small_sum = sum_sides(small_sum, sides)
    router_grad = small_sum[: router_flat.shape[1]].reshape(w_router.shape)
    gains_grad = small_sum[router_flat.shape[1] :].reshape(norm_gains.shape)
    qkv_grad = sum_sides(total_of(qkv_sums), sides)
    out_grad = sum_sides(total_of(out_sums), sides)
    new_gains, new_gains_moment, new_gains_square = adam_update(
        norm_gains, gains_moment, gains_square, gains_grad, rate_gains, 0.0
    )
    new_qkv, new_qkv_moment, new_qkv_square = adam_update(
        w_qkv, qkv_moment, qkv_square, qkv_grad, rate_qkv, decay_matrix
    )
    new_out, new_out_moment, new_out_square = adam_update(
        w_out, out_moment, out_square, out_grad, rate_out, decay_matrix
    )
    new_router, new_router_moment, new_router_square = adam_update(
        w_router, router_moment, router_square, router_grad, rate_router, decay_matrix
    )
    new_gate_up, new_gate_up_moment, new_gate_up_square = adam_update(
        w_gate_up, gate_up_moment, gate_up_square, gate_up_grad, rate_gate_up, decay_matrix
    )
    new_down, new_down_moment, new_down_square = adam_update(
        w_down, down_moment, down_square, down_grad, rate_down, decay_matrix
    )
    return (
        block_out,
        input_grad,
        gains_grad,
        qkv_grad,
        out_grad,
        router_grad,
        gate_up_grad,
        down_grad,
        new_gains,
        new_gains_moment,
        new_gains_square,
        new_qkv,
        new_qkv_moment,
        new_qkv_square,
        new_out,
        new_out_moment,
        new_out_square,
        new_router,
        new_router_moment,
        new_router_square,
        new_gate_up,
        new_gate_up_moment,
        new_gate_up_square,
        new_down,
        new_down_moment,
        new_down_square,
    )


def solution(mesh):
    return jax.shard_map(
        functools.partial(local, mesh.shape[DP], mesh.shape[SHARD]),
        mesh=mesh,
        in_specs=(
            P((DP, SHARD), None),
            P(DP, SHARD),
            P((DP, SHARD), None),
            P((DP, SHARD), None),
            P(None, DP),
            P(None, DP),
            P(None, DP),
            P(DP, None),
            P(DP, None),
            P(DP, None),
            P(DP, None),
            P(DP, None),
            P(DP, None),
            P(DP, None),
            P(DP, None),
            P(DP, None),
            P(DP, SHARD, None),
            P(DP, SHARD, None),
            P(DP, SHARD, None),
            P(DP, SHARD, None),
            P(DP, SHARD, None),
            P(DP, SHARD, None),
        ),
        out_specs=(
            P((DP, SHARD), None),
            P((DP, SHARD), None),
            P(None, DP),
            P(DP, None),
            P(DP, None),
            P(DP, None),
            P(DP, SHARD, None),
            P(DP, SHARD, None),
            P(None, DP),
            P(None, DP),
            P(None, DP),
            P(DP, None),
            P(DP, None),
            P(DP, None),
            P(DP, None),
            P(DP, None),
            P(DP, None),
            P(DP, None),
            P(DP, None),
            P(DP, None),
            P(DP, SHARD, None),
            P(DP, SHARD, None),
            P(DP, SHARD, None),
            P(DP, SHARD, None),
            P(DP, SHARD, None),
            P(DP, SHARD, None),
        ),
        check_vma=False,
    )
```
